32 devices in a mesh: row: 8 (over z, y), col: 4 (over x, core).
Axes of the slice: x: 2, y: 2, z: 4, core: 2. Of those that a mesh axis runs over, the one named last changes fastest.
Arguments:
- activations: bfloat16 [512, 28672], P('col', 'row'), may hold values from -36 to 36
- output_gradient: bfloat16 [512, 8192], P('row', 'col'), may hold values from -6 to 6
- frozen_weight: bfloat16 [28672, 8192], P('row', 'col'), may hold values from -0.0390625 to 0.0390625
- sparsity_mask_pattern: int32 [7168, 8192], P('row', 'col'), may hold values from 0 to 5
- adapter_left_factor: bfloat16 [28672, 16], P('row'), may hold values from -0.19921875 to 0.19921875
- adapter_right_factor: bfloat16 [16, 8192], P(None, 'col'), may hold values from -0.359375 to 0.359375
Outputs:
- input_grad: bfloat16 [512, 28672], P('col', 'row')
- left_grad: float32 [28672, 16], P('row')
- right_grad: float32 [16, 8192], P(None, 'col')
The draws below stay inside these ranges and needn't reach their ends.
Inputs may be any that keep to these rules, and one draw needn't show every extreme that they name: `sparsity_mask_pattern`: a pattern number of the 2:4 mask.
All inputs are finite; a program needn't handle non-finite values.
Results may differ from the reference program's by a relative error of at most 0.005.
Values may be sent and summed in bfloat16 or wider, within the bound.
No kernel may reach another device: no remote copies, remote signals or barrier semaphores. Data moves between devices by JAX's collectives and lax.ppermute only.
A program may use at most 192 MiB of HBM per device.

```python
import jax
import jax.numpy as jnp
from jax import lax

MODEL_WIDTH = 8192
HIDDEN_UNITS = 28672
ADAPTER_RANK = 16
TOKENS = 512
N_ROW = 8


def plant(drawn, stream_key, least, high):
    dims = drawn.shape
    place = [jax.random.randint(jax.random.fold_in(stream_key, axis), (), 0, dims[axis]) for axis in range(len(dims))]
    drawn = drawn.at[tuple(place)].set(least)
    longest = dims.index(max(dims))
    place[longest] = (place[longest] + 1) % dims[longest]
    return drawn.at[tuple(place)].set(high)


def raised(drawn, key, source, target, shards_of, factor):
    owner, partner = [(jnp.arange(drawn.shape[position]) // (drawn.shape[position] // shards_of)).reshape([-1 if axis == position else 1 for axis in range(drawn.ndim)]) for position in (source, target)]
    chosen = jax.random.permutation(key, shards_of)[partner]
    strong = (owner == chosen) | (owner == (partner + shards_of // 2) % shards_of)
    return jnp.where(strong, factor * drawn, drawn)


def levels(stream_key, shape, split, smallest, largest):
    factor_of, own = 1.0, jax.random.fold_in(stream_key, 6)
    for dim, blocks in split:
        steps = jnp.exp(jax.random.uniform(jax.random.fold_in(own, dim), (blocks,), jnp.float32, smallest / len(split), largest / len(split)))
        factor_of = factor_of * jnp.repeat(steps, shape[dim] // blocks).reshape([-1 if axis == dim else 1 for axis in range(len(shape))])
    return factor_of


def noise(key, extent, spread, reach, shards=(), dtype=jnp.bfloat16):
    drawn = spread * jax.random.normal(key, extent, jnp.float32)
    if shards:
        drawn = drawn * levels(key, extent, shards, -0.22, 0.18)
    return jnp.clip(drawn, -reach, reach).astype(dtype)


def bell_draw_with(key, dims, width, most, cuts, heavy, held_as=jnp.bfloat16):
    drawn = width * jax.random.normal(key, dims, jnp.float32)
    if cuts:
        drawn = drawn * levels(key, dims, cuts, -0.22, 0.18)
    return jnp.clip(raised(drawn, jax.random.fold_in(key, 3), *heavy), -most, most).astype(held_as)


def setup_inputs(seed: int = 0) -> dict:
    streams_of = jax.random.split(jax.random.key(seed), 7)
    activations = noise(streams_of[0], (TOKENS, HIDDEN_UNITS), 6.0, 36.0, ((0, 4), (1, 8)))
    output_gradient = bell_draw_with(streams_of[1], (TOKENS, MODEL_WIDTH), 1.0, 6.0, ((0, 8), (1, 4)), (1, 0, 8, 2.0))
    frozen_weight = noise(streams_of[2], (HIDDEN_UNITS, MODEL_WIDTH), (3 * HIDDEN_UNITS // 4) ** -0.5, 0.0390625, ((0, 8), (1, 4)))
    sparsity_mask_pattern = plant(jax.random.randint(streams_of[3], (HIDDEN_UNITS // 4, MODEL_WIDTH), 0, 6), jax.random.fold_in(streams_of[3], 1), 0, 5).astype(jnp.int32)
    adapter_left_factor = noise(streams_of[4], (HIDDEN_UNITS, ADAPTER_RANK), 0.032, 0.19921875, ((0, 8),))
    adapter_right_factor = noise(streams_of[5], (ADAPTER_RANK, MODEL_WIDTH), 0.06, 0.359375, ((1, 4),))
    return dict(activations=activations, output_gradient=output_gradient, frozen_weight=frozen_weight, sparsity_mask_pattern=sparsity_mask_pattern, adapter_left_factor=adapter_left_factor, adapter_right_factor=adapter_right_factor)


PAIRS = ((0, 1), (0, 2), (0, 3), (1, 2), (1, 3), (2, 3))
ADAPTER_SCALE = 2.0


def expand_mask(code):
    groups = []
    for column in range(4):
        kept = jnp.zeros(code.shape, jnp.float32)
        for pattern in range(6):
            if column in PAIRS[pattern]:
                kept = kept + (code == pattern).astype(jnp.float32)
        groups.append(kept)
    stacked = jnp.stack(groups, axis=1)
    return stacked.reshape(code.shape[0] * 4, code.shape[1])


def reference(activations, output_gradient, frozen_weight, sparsity_mask_pattern, adapter_left_factor, adapter_right_factor):
    block_list = N_ROW
    width_extent = HIDDEN_UNITS // block_list
    act_blocks = activations.reshape(TOKENS, block_list, width_extent).transpose(1, 0, 2)
    weight_blocks = frozen_weight.reshape(block_list, width_extent, MODEL_WIDTH)
    code_blocks = sparsity_mask_pattern.reshape(block_list, width_extent // 4, MODEL_WIDTH)
    left_block_list = adapter_left_factor.reshape(block_list, width_extent, ADAPTER_RANK)

    def one_block(carry, inputs):
        act_piece, weight_piece, code_piece, left_block_slice = inputs
        masked = expand_mask(code_piece)
        low_rank_update = jnp.dot(left_block_slice, adapter_right_factor, preferred_element_type=jnp.float32)
        merged = (masked * (weight_piece.astype(jnp.float32) + ADAPTER_SCALE * low_rank_update)).astype(jnp.bfloat16)
        input_piece = lax.dot_general(output_gradient, merged, (((1,), (1,)), ((), ())), preferred_element_type=jnp.float32).astype(jnp.bfloat16)
        weight_grad = lax.dot_general(act_piece, output_gradient, (((0,), (0,)), ((), ())), preferred_element_type=jnp.float32)
        pruned_gradient = (masked * weight_grad / TOKENS).astype(jnp.bfloat16)
        left_slice_gradient = ADAPTER_SCALE * lax.dot_general(pruned_gradient, adapter_right_factor, (((1,), (1,)), ((), ())), preferred_element_type=jnp.float32)
        carry = carry + ADAPTER_SCALE * lax.dot_general(left_block_slice, pruned_gradient, (((0,), (0,)), ((), ())), preferred_element_type=jnp.float32)
        return carry, (input_piece, left_slice_gradient)

    start_carry = jnp.zeros((ADAPTER_RANK, MODEL_WIDTH), jnp.float32)
    right_grad, outputs = lax.scan(one_block, start_carry, (act_blocks, weight_blocks, code_blocks, left_block_list))
    input_parts, left_parts = outputs
    input_grad = input_parts.transpose(1, 0, 2).reshape(TOKENS, HIDDEN_UNITS)
    left_grad = left_parts.reshape(HIDDEN_UNITS, ADAPTER_RANK)
    return input_grad, left_grad, right_grad
```

```python
import functools

import jax
import jax.numpy as jnp
from jax import lax
from jax.experimental import pallas as pl
from jax.experimental.pallas import tpu as pltpu
from jax.sharding import PartitionSpec as P

PAIRS = ((0, 1), (0, 2), (0, 3), (1, 2), (1, 3), (2, 3))
KEPT = tuple(sum(1 << p for p, pair in enumerate(PAIRS) if j in pair) for j in range(4))
ADAPTER_SCALE = 2.0
LANES = 128
F32, BF16 = jnp.float32, jnp.bfloat16
VMEM_BYTES = 56 * 1024 * 1024


def tile_of(extent, most):
    tile = most
    while extent % tile:
        tile -= LANES
    return tile


def params():
    return pltpu.CompilerParams(vmem_limit_bytes=VMEM_BYTES)


def cost(flops, nbytes):
    return pl.CostEstimate(flops=flops, bytes_accessed=nbytes, transcendentals=0)


def merge_kernel(code_ref, w_ref, lt_ref, r_ref, merged_ref, mask_ref, expand):
    groups, cols = code_ref.shape
    rows = 4 * groups
    for c in range(cols // LANES):
        code = code_ref[:, pl.ds(c * LANES, LANES)]
        for j in range(4):
            kept = lax.shift_right_logical(jnp.full(code.shape, KEPT[j], jnp.int32), code) & 1
            expand[pl.ds(c * rows + j, groups, stride=4), :] = kept.astype(F32)
    update = lax.dot_general(
        lt_ref[...] * ADAPTER_SCALE, r_ref[...], (((0,), (0,)), ((), ())), preferred_element_type=F32
    )
    for c in range(cols // LANES):
        at = pl.ds(c * LANES, LANES)
        mask = expand[pl.ds(c * rows, rows), :]
        whole = w_ref[:, at].astype(F32) + update[:, c * LANES : (c + 1) * LANES]
        merged_ref[:, at] = (mask * whole).astype(BF16)
        mask_ref[:, at] = mask.astype(BF16)


def merge(code, w, lt, r):
    hid, cols = w.shape
    rank = r.shape[0]
    th = tile_of(hid, 512)
    return pl.pallas_call(
        merge_kernel,
        grid=(hid // th,),
        in_specs=[
            pl.BlockSpec((th // 4, cols), lambda i: (i, 0)),
            pl.BlockSpec((th, cols), lambda i: (i, 0)),
            pl.BlockSpec((rank, th), lambda i: (0, i)),
            pl.BlockSpec((rank, cols), lambda i: (0, 0)),
        ],
        out_specs=[pl.BlockSpec((th, cols), lambda i: (i, 0))] * 2,
        out_shape=[jax.ShapeDtypeStruct((hid, cols), BF16)] * 2,
        scratch_shapes=[pltpu.VMEM((th * cols // LANES, LANES), F32)],
        compiler_params=params(),
        cost_estimate=cost(2 * hid * cols * rank, 9 * hid * cols),
        name="merge",
    )(code, w, lt, r)


def join_kernel(at_ref, *refs):
    *blocks, out_ref = refs
    tall = blocks[0].shape[0]
    for k, block in enumerate(blocks):
        out_ref[pl.ds(pl.multiple_of(at_ref[k], tall), tall), :] = block[...]


def join(at, blocks):
    tall, cols = blocks[0].shape
    n = len(blocks)
    tc = tile_of(cols, 512)
    return pl.pallas_call(
        join_kernel,
        grid_spec=pltpu.PrefetchScalarGridSpec(
            num_scalar_prefetch=1,
            grid=(cols // tc,),
            in_specs=[pl.BlockSpec((tall, tc), lambda i, at: (0, i))] * n,
            out_specs=pl.BlockSpec((n * tall, tc), lambda i, at: (0, i)),
        ),
        out_shape=jax.ShapeDtypeStruct((n * tall, cols), BF16),
        compiler_params=params(),
        cost_estimate=cost(0, 4 * n * tall * cols),
        name="join",
    )(at, *blocks)


def back_kernel(dy_ref, m_ref, keep_ref, send_ref, *, tall):
    p = lax.dot_general(dy_ref[...], m_ref[...], (((1,), (1,)), ((), ())), preferred_element_type=F32)
    for k in range(p.shape[0] // tall):
        out_ref = send_ref if k % 2 else keep_ref
        out_ref[pl.ds(k // 2 * tall, tall), :] = p[k * tall : (k + 1) * tall].astype(out_ref.dtype)


def back(dy, merged, first, count, tall):
    tokens, cols = dy.shape
    th = tile_of(count, 512)
    return pl.pallas_call(
        functools.partial(back_kernel, tall=tall),
        grid=(count // th,),
        in_specs=[
            pl.BlockSpec((tokens, cols), lambda i: (0, 0)),
            pl.BlockSpec((th, cols), lambda i: (i + first // th, 0)),
        ],
        out_specs=[pl.BlockSpec((tokens // 2, th), lambda i: (0, i))] * 2,
        out_shape=[
            jax.ShapeDtypeStruct((tokens // 2, count), F32),
            jax.ShapeDtypeStruct((tokens // 2, count), BF16),
        ],
        compiler_params=params(),
        cost_estimate=cost(2 * tokens * cols * count, 2 * cols * count),
        name="back",
    )(dy, merged)


def adapter_kernel(*refs, parts, scale):
    acts = refs[:parts]
    dy_ref, mask_ref, lt_ref, r_ref, left_in, left_ref, right_ref = refs[parts:]
    act = jnp.concatenate([a[...] for a in acts], axis=0)
    g = lax.dot_general(act, dy_ref[...], (((0,), (0,)), ((), ())), preferred_element_type=F32)
    g = (g * scale).astype(BF16) * mask_ref[...]
    left_ref[...] = left_in[...] + lax.dot_general(
        r_ref[...] * ADAPTER_SCALE, g, (((1,), (1,)), ((), ())), preferred_element_type=F32
    )
    right = lax.dot_general(
        lt_ref[...] * ADAPTER_SCALE, g, (((1,), (0,)), ((), ())), preferred_element_type=F32
    )

    @pl.when(pl.program_id(0) == 0)
    def _():
        right_ref[...] = right

    @pl.when(pl.program_id(0) != 0)
    def _():
        right_ref[...] += right


def adapter(acts, dy, mask, lt, r, left, first, count):
    rank, hid = lt.shape
    tall = acts[0].shape[0]
    tokens = dy.shape[0]
    th = tile_of(hid, 512)
    c = first // count
    return pl.pallas_call(
        functools.partial(adapter_kernel, parts=len(acts), scale=1.0 / tokens),
        grid=(hid // th,),
        in_specs=[pl.BlockSpec((tall, th), lambda i: (0, i))] * len(acts)
        + [
            pl.BlockSpec((tokens, count), lambda i: (0, c)),
            pl.BlockSpec((th, count), lambda i: (i, c)),
            pl.BlockSpec((rank, th), lambda i: (0, i)),
            pl.BlockSpec((rank, count), lambda i: (0, c)),
            pl.BlockSpec((rank, th), lambda i: (0, i)),
        ],
        out_specs=[
            pl.BlockSpec((rank, th), lambda i: (0, i)),
            pl.BlockSpec((rank, count), lambda i: (0, 0)),
        ],
        out_shape=[
            jax.ShapeDtypeStruct((rank, hid), F32),
            jax.ShapeDtypeStruct((rank, count), F32),
        ],
        compiler_params=params(),
        cost_estimate=cost(2 * hid * count * (tokens + 4 * rank), 2 * hid * count),
        name="adapter",
    )(*acts, dy, mask, lt, r, left)


def exchange(x, axis, size, bit):
    return lax.ppermute(x, axis, [(i, i ^ bit) for i in range(size)])


def per_device(act, dy, weight, code, left_factor, right_factor, *, rows, cols):
    bits = [1 << b for b in range(cols.bit_length() - 1)]
    hid, width = weight.shape
    tall, short = act.shape[0], dy.shape[0]
    tokens = tall * cols
    lt = left_factor.T

    parts = {0: act}
    for bit in reversed(bits):
        parts.update({k | bit: exchange(v, "col", cols, bit) for k, v in list(parts.items())})
    acts = [parts[k] for k in range(cols)]

    ring = list(range(0, rows, 2)) + list(range(1, rows, 2))[::-1]
    up = [(ring[i], ring[(i + 1) % rows]) for i in range(rows)]
    down = [(b, a) for a, b in up]
    blocks = {0: dy}
    for step in range(1, rows // 2 + 1):
        blocks[-step] = lax.ppermute(blocks[1 - step], "row", up)
        if step < rows - step:
            blocks[step] = lax.ppermute(blocks[step - 1], "row", down)
    me = lax.axis_index("row")
    place = jnp.where(me % 2 == 0, me // 2, rows - 1 - me // 2)
    steps = sorted(blocks)
    spot = (place + jnp.array(steps, jnp.int32)) % rows
    source = jnp.where(spot < (rows + 1) // 2, 2 * spot, 2 * (rows - 1 - spot) + 1)
    start = source * short
    at = ((start // tall) ^ lax.axis_index("col")) * tall + start % tall

    merged, mask = merge(code, weight, lt, right_factor)
    all_dy = join(at.astype(jnp.int32), [blocks[s] for s in steps])

    pieces = []
    n_back = 2
    for i in range(n_back):
        count = hid // n_back
        keep, send = back(all_dy, merged, i * count, count, tall)
        for bit in bits:
            total = keep.reshape(-1, tall, count) + exchange(send, "col", cols, bit).reshape(-1, tall, count).astype(F32)
            keep, send = total[0::2], total[1::2].astype(BF16)
        pieces.append(keep[0].astype(BF16))
    input_grad = jnp.concatenate(pieces, axis=1)

    left = jnp.zeros(lt.shape, F32)
    rights = []
    n_col = 2
    for i in range(n_col):
        count = width // n_col
        left, right = adapter(acts, all_dy, mask, lt, right_factor, left, i * count, count)
        for b in range(rows.bit_length() - 1):
            right = right + exchange(right, "row", rows, 1 << b)
        rights.append(right)
    for bit in bits:
        left = left + exchange(left, "col", cols, bit)
    return input_grad, left.T, jnp.concatenate(rights, axis=1)


def solution(mesh):
    in_specs = (
        P("col", "row"),
        P("row", "col"),
        P("row", "col"),
        P("row", "col"),
        P("row", None),
        P(None, "col"),
    )
    out_specs = (P("col", "row"), P("row", None), P(None, "col"))
    body = functools.partial(per_device, rows=mesh.shape["row"], cols=mesh.shape["col"])
    return jax.shard_map(body, mesh=mesh, in_specs=in_specs, out_specs=out_specs, check_vma=False)
```
